32 devices in a mesh: row: 8 (over z, x), col: 4 (over y, core).
Axes of the slice: x: 2, y: 2, z: 4, core: 2. Of those that a mesh axis runs over, the one named last changes fastest.
Arguments:
- diag_inverse: bfloat16 [2, 8192, 8192], P(None, 'col', 'row'), as said below
- panel_rhs: bfloat16 [2, 8192, 128], P(None, 'row'), may hold values from -6 to 6
- below: bfloat16 [2, 22528, 8192], P(None, 'row', 'col'), may hold values from -0.03125 to 0.03125
- row_ids: int32 [2, 176], P(None, 'row'), may hold values from 0 to 256, as said below
- ancestor_rhs: bfloat16 [24576, 128], P(('row', 'col')), may hold values from -6 to 6
- ancestor_solution: bfloat16 [24576, 128], P(('row', 'col')), may hold values from -6 to 6
Outputs:
- solution: bfloat16 [2, 8192, 128], P(None, ('row', 'col'))
- rhs_updated: bfloat16 [24576, 128], P(('row', 'col'))
The draws below stay inside these ranges and needn't reach their ends.
Inputs may be any that keep to these rules, and one draw needn't show every extreme that they name: diag_inverse[p] is lower triangular with a positive diagonal. `row_ids`: slots 22 r to 22 r + 21 of either panel belong to the r-th index of row. Each holds 256 (empty) or a later block row that this index owns: for panel 0 a panel-1 block row in [r * 8, r * 8 + 8) or a value in [64 + r * 24, 64 + r * 24 + 24); for panel 1 only the latter. Live ids of one panel are distinct. In each panel some index of row has all 22 slots live.
All inputs are finite; a program needn't handle non-finite values.
Results may differ from the reference program's by a relative error of at most 0.017.
Values may be sent and summed in bfloat16 or wider, within the bound.
A program may use at most 128 MiB of HBM per device.

```python
import jax
import jax.numpy as jnp
from jax import lax

BS = 128
NRHS = 128
PW = 64
CAP = 22
NA_R = 24
COLS = 8192
NA = 192
SLOTS = 176
LATER = 256
N_ROW = 8


def draw_diag_inverse(key, part):
    noise_key, scale_key = jax.random.split(key)
    row_grid = lax.broadcasted_iota(jnp.int32, (2, COLS, COLS), 1)
    col_grid = lax.broadcasted_iota(jnp.int32, (2, COLS, COLS), 2)
    lower_part = jax.random.normal(noise_key, (2, COLS, COLS), jnp.float32)
    diagonal = jax.random.uniform(scale_key, (2, COLS, 1), jnp.float32, 0.7, 1.4)
    values = jnp.where(row_grid > col_grid, lower_part * COLS ** (-0.5), 0.0)
    values = values + jnp.where(row_grid == col_grid, diagonal, 0.0)
    return values.astype(jnp.bfloat16)


def draw_row_ids(key, part):
    panels = []
    pw_rows = PW // N_ROW
    for panel_index in range(2):
        panel_key = jax.random.fold_in(key, 7 + panel_index)
        full_key, count_key, owner_key = jax.random.split(panel_key, 3)
        full_owner = jax.random.randint(full_key, (), 0, N_ROW)
        low_owner = (full_owner + 1) % N_ROW
        owners = jnp.arange(N_ROW, dtype=jnp.int32)
        counts = jax.random.randint(count_key, (N_ROW,), CAP // 4, CAP + 1)
        counts = jnp.where(owners == full_owner, CAP, jnp.where(owners == low_owner, CAP // 4, counts))
        panel_extra = pw_rows if panel_index == 0 else 0
        candidates = panel_extra + NA_R

        def one_owner(owner_seed, owner_index, live_count):
            pick_key, place_key = jax.random.split(owner_seed)
            picked = jax.random.permutation(pick_key, candidates)[:CAP]
            position = jax.random.permutation(place_key, CAP)
            slot_ids = jnp.where(picked < panel_extra, owner_index * pw_rows + picked, PW + owner_index * NA_R + picked - panel_extra)
            return jnp.where(position < live_count, slot_ids, PW + NA_R * N_ROW)
        owner_keys = jax.random.split(owner_key, N_ROW)
        slots_all = jax.vmap(one_owner)(owner_keys, owners, counts)
        panels.append(slots_all.reshape(N_ROW * CAP))
    return jnp.stack(panels).astype(jnp.int32)


def level_of(rng, shape, cuts, least, largest):
    def one(dim, blocks):
        draws = jax.random.uniform(jax.random.fold_in(jax.random.fold_in(rng, 6), dim), (blocks,), jnp.float32, least / len(cuts), largest / len(cuts))
        return jnp.repeat(jnp.exp(draws), shape[dim] // blocks).reshape((-1,) + (1,) * (len(shape) - dim - 1))

    loudness = one(*cuts[0])
    for cut in cuts[1:]:
        loudness = loudness * one(*cut)
    return loudness


def scatter_about(rng, extent, deviation, most, cuts=(), held_as=jnp.bfloat16):
    level = level_of(rng, extent, cuts, -0.22, 0.18) if cuts else 1.0
    entries = jax.random.normal(rng, extent, jnp.float32) * deviation * level
    return jnp.minimum(jnp.maximum(entries, -most), most).astype(held_as)


def setup_inputs(seed: int = 0) -> dict:
    key_of = jax.random.split(jax.random.key(seed), 7)
    return {
        "diag_inverse": draw_diag_inverse(jax.random.fold_in(key_of[6], 71), 0),
        "panel_rhs": scatter_about(key_of[1], (2, COLS, NRHS), 1.0, 6.0, ((1, 8),)),
        "below": scatter_about(key_of[2], (2, SLOTS * BS, COLS), (4 * PW * BS) ** -0.5, 0.03125, ((1, 8), (2, 4))),
        "row_ids": draw_row_ids(jax.random.fold_in(key_of[6], 71), 0),
        "ancestor_rhs": scatter_about(key_of[4], (NA * BS, NRHS), 1.0, 6.0, ((0, 32),)),
        "ancestor_solution": scatter_about(key_of[5], (NA * BS, NRHS), 1.0, 6.0, ((0, 32),)),
    }


def slot_terms(factor_panel, solved, slot_ids):
    owner_blocks = factor_panel.reshape(N_ROW, CAP * BS, COLS)
    products = lax.map(lambda owner_rows: jnp.dot(owner_rows, solved, preferred_element_type=jnp.float32), owner_blocks)
    products = products.reshape(SLOTS, BS, NRHS)
    summed = jax.ops.segment_sum(products, slot_ids, num_segments=LATER + 1)
    return summed[:LATER]


def back_terms(factor_panel, known, slot_ids):
    gathered = known[slot_ids].reshape(N_ROW, CAP * BS, NRHS)
    owner_blocks = factor_panel.reshape(N_ROW, CAP * BS, COLS)

    def owner_product(pair_in):
        return lax.dot_general(pair_in[0], pair_in[1], (((0,), (0,)), ((), ())), preferred_element_type=jnp.float32)

    products = lax.map(owner_product, (owner_blocks, gathered))
    return jnp.sum(products, axis=0)


def reference(diag_inverse, panel_rhs, below, row_ids, ancestor_rhs, ancestor_solution):
    forward_zero = jnp.dot(diag_inverse[0], panel_rhs[0], preferred_element_type=jnp.float32).astype(jnp.bfloat16)
    later_zero = slot_terms(below[0], forward_zero, row_ids[0])
    panel_part = later_zero[:PW].reshape(COLS, NRHS)
    panel_one_rhs = (panel_rhs[1].astype(jnp.float32) - panel_part).astype(jnp.bfloat16)
    forward_one = jnp.dot(diag_inverse[1], panel_one_rhs, preferred_element_type=jnp.float32).astype(jnp.bfloat16)
    later_one = slot_terms(below[1], forward_one, row_ids[1])
    update = (later_zero[PW:] + later_one[PW:]).reshape(NA * BS, NRHS)
    rhs_updated = (ancestor_rhs.astype(jnp.float32) - update).astype(jnp.bfloat16)
    ancestor_blocks = ancestor_solution.reshape(NA, BS, NRHS)
    empty_panel = jnp.zeros((PW, BS, NRHS), jnp.bfloat16)
    empty_slot = jnp.zeros((1, BS, NRHS), jnp.bfloat16)
    known_one = jnp.concatenate([empty_panel, ancestor_blocks, empty_slot], axis=0)
    back_one_terms = back_terms(below[1], known_one, row_ids[1])
    back_one_rhs = (forward_one.astype(jnp.float32) - back_one_terms).astype(jnp.bfloat16)
    solution_one = jnp.dot(diag_inverse[1].T, back_one_rhs, preferred_element_type=jnp.float32).astype(jnp.bfloat16)
    known_zero = jnp.concatenate([solution_one.reshape(PW, BS, NRHS), ancestor_blocks, empty_slot], axis=0)
    back_zero_terms = back_terms(below[0], known_zero, row_ids[0])
    back_zero_rhs = (forward_zero.astype(jnp.float32) - back_zero_terms).astype(jnp.bfloat16)
    solution_zero = jnp.dot(diag_inverse[0].T, back_zero_rhs, preferred_element_type=jnp.float32).astype(jnp.bfloat16)
    solution = jnp.stack([solution_zero, solution_one])
    return solution, rhs_updated
```

```python
import functools

import jax
import jax.numpy as jnp
from jax import lax
from jax.experimental import pallas as pl
from jax.experimental.pallas import tpu as pltpu
from jax.sharding import PartitionSpec as P

MESH = pl.DeviceIdType.MESH
BF = jnp.bfloat16
F32 = jnp.float32


def sizes_of(n, m, diag, panel_rhs, below, row_ids, ancestor_rhs):
    z = {}
    z["n"], z["m"] = n, m
    z["nz"] = n // 2
    z["cc"], z["p"] = diag.shape[1], diag.shape[2]
    z["nrhs"] = panel_rhs.shape[2]
    z["cap"] = row_ids.shape[1]
    z["bs"] = below.shape[1] // z["cap"]
    z["b"] = z["cc"] // n
    z["q"] = z["p"] // m
    z["a"] = ancestor_rhs.shape[0]
    z["ab"] = z["a"] // z["bs"]
    z["na"] = z["ab"] * m
    z["pb"] = z["p"] // z["bs"]
    z["pw"] = z["cc"] * m // z["bs"]
    return z


def kernel(
    z, ids_hbm, d_hbm, prhs_hbm, b_hbm, arhs_hbm, asol_hbm, sol_hbm, upd_hbm,
    ids, idx, vd0, vd1, vb0, vb1, prhs, arhs, sol, upd, known, known_t, vt, slots, acc_t,
    acc_p, acc_f, acc_s, b1_mine,
    part_b1, full_f1, wide, part_f0, part_f1, part_b0, full_f0, full_b1, full_b0,
    xr, zs, zr, xr1, zs1, zr1, part_p, full_p, part_s1, full_s1, part_s0, part_u,
    cl, ys, yl, cr, cru,
    lsem, dsem, osem, ssem, rsem,
):
    n, m, nz, b, q = z["n"], z["m"], z["nz"], z["b"], z["q"]
    cc, cap, bs, nrhs, na, pb = z["cc"], z["cap"], z["bs"], z["nrhs"], z["na"], z["pb"]
    ab, a, p = z["ab"], z["a"], z["p"]
    me = lax.axis_index("row")
    mc = lax.axis_index("col")
    par = lax.rem(me, 2)
    zi = me // 2
    partner = me + 1 - 2 * par
    core = lax.rem(mc, 2)
    yi = mc // 2
    ny = m // 2
    twin = mc + 1 - 2 * core
    o_pan, o_l0, o_l1, o_p0, o_p1 = 0, pb, pb + na, pb + 2 * na, pb + 2 * na + cap

    counter = [0]
    pending = []

    def send(src, dst, axis, place, slot):
        cp = pltpu.make_async_remote_copy(
            src_ref=src, dst_ref=dst, send_sem=ssem.at[slot], recv_sem=rsem.at[slot],
            device_id={axis: place}, device_id_type=MESH,
        )
        cp.start()
        pending.append(cp)
        return cp

    def settle(count):
        for cp in pending[:count]:
            cp.wait_send()
        del pending[:count]

    def take(count):
        base = counter[0]
        counter[0] += count
        return base

    def span(block, size):
        return pl.ds(pl.multiple_of(block * size, size), size)

    def rows(ref, block, size):
        return ref.at[span(block, size)]

    def get(ref, block, size):
        return ref[span(block, size), :]

    def put(ref, block, size, value):
        ref[span(block, size), :] = value

    class RowSum:
        def __init__(self, part, size, xr, zs, zr):
            self.part, self.size = part, size
            self.xr, self.zs, self.zr = xr, zs, zr
            self.xk, self.zk = take(nz), take(nz)
            self.xc, self.zc = {}, {}

        def send_x(self, j):
            zd = lax.rem(zi + j, nz)
            self.xc[j] = send(
                rows(self.part, zd * 2 + 1 - par, self.size), self.xr.at[j], "row", partner,
                self.xk + j,
            )

        def forward(self):
            for j in order[:-1]:
                zd = lax.rem(zi + j, nz)
                self.xc[j].wait_recv()
                mine = get(self.part, zd * 2 + par, self.size)
                self.zs[j] = (mine.astype(F32) + self.xr[j].astype(F32)).astype(BF)
                self.zc[j] = send(
                    self.zs.at[j], self.zr.at[j], "row", zd * 2 + par, self.zk + j
                )

        def finish(self):
            self.xc[0].wait_recv()
            total = get(self.part, me, self.size).astype(F32) + self.xr[0].astype(F32)
            for j in order[:-1]:
                self.zc[j].wait_recv()
                total = total + self.zr[j].astype(F32)
            return total

    class RowGather:
        def __init__(self, full, size):
            self.full, self.size = full, size
            self.xk, self.zk = take(nz), take(nz)
            self.xc, self.zc = {}, {}

        def start(self):
            mine = rows(self.full, me, self.size)
            for j in order[:-1]:
                self.zc[j] = send(mine, mine, "row", lax.rem(zi + j, nz) * 2 + par, self.zk + j)
            self.xc[0] = send(mine, mine, "row", partner, self.xk)

        def forward(self):
            for j in order[:-1]:
                self.zc[j].wait_recv()
                theirs = rows(self.full, lax.rem(zi + nz - j, nz) * 2 + par, self.size)
                self.xc[j] = send(theirs, theirs, "row", partner, self.xk + j)

        def finish(self):
            for j in range(nz):
                self.xc[j].wait_recv()

    class ColSum:
        def __init__(self, part, landing, size):
            self.part, self.landing, self.size = part, landing, size
            self.s = take(m)
            self.c = {}

        def send_to(self, d):
            place = lax.rem(mc + d, m)
            self.c[d] = send(
                rows(self.part, place, self.size), self.landing.at[d], "col", place, self.s + d
            )

        def finish(self):
            total = get(self.part, mc, self.size).astype(F32)
            for d in range(1, m):
                self.c[d].wait_recv()
                total = total + self.landing[d].astype(F32)
            return total

    class ColGather:
        def __init__(self, full, size):
            self.full, self.size = full, size
            self.s, self.t = take(ny), take(ny)
            self.y, self.c = {}, {}

        def start(self):
            mine = rows(self.full, mc, self.size)
            for d in range(1, ny):
                place = lax.rem(yi + d, ny) * 2 + core
                self.y[d] = send(mine, mine, "col", place, self.s + d)
            self.c[0] = send(mine, mine, "col", twin, self.t)

        def forward(self):
            for d in range(1, ny):
                self.y[d].wait_recv()
                theirs = rows(self.full, lax.rem(yi + ny - d, ny) * 2 + core, self.size)
                self.c[d] = send(theirs, theirs, "col", twin, self.t + d)

        def finish(self):
            for d in range(ny):
                self.c[d].wait_recv()

    hp = p // 4

    class ColReduce:
        def __init__(self, part, full, twin_in, out, landing):
            self.part, self.full, self.twin_in = part, full, twin_in
            self.out, self.landing = out, landing
            self.s = take(2 + ny)
            self.c = {}

        def send_twin(self):
            self.t = send(
                rows(self.part, 1 - core, hp), self.twin_in, "col", twin, self.s
            )

        def send_y(self, mine):
            self.t.wait_recv()
            self.out[...] = (mine + self.twin_in[...].astype(F32)).astype(BF)
            for d in range(1, ny):
                place = lax.rem(yi + d, ny) * 2 + core
                self.c[d] = send(self.out, self.landing.at[d], "col", place, self.s + 1 + d)

        def total(self):
            total = self.out[...].astype(F32)
            for d in range(1, ny):
                self.c[d].wait_recv()
                total = total + self.landing[d].astype(F32)
            return total

        def share(self, value):
            put(self.full, core, hp, value)
            mine = rows(self.full, core, hp)
            self.g = send(mine, mine, "col", twin, self.s + 1)

        def finish(self):
            self.g.wait_recv()

    hb, hq, hn = b // 2, q // 2, nrhs // 2

    def pack(value, size):
        blocks = value.reshape(-1, size, hn)
        half = size // 2
        both = jnp.concatenate([blocks[:, :half], blocks[:, half:]], axis=2)
        return both.reshape(-1, nrhs)

    def unpack(value, size):
        half = size // 2
        blocks = value.astype(F32).reshape(-1, half, nrhs)
        both = jnp.concatenate([blocks[:, :, :hn], blocks[:, :, hn:]], axis=1)
        return both.reshape(-1, hn)

    def part_of(value, h):
        return value[:, h * hn:(h + 1) * hn]

    order = list(range(1, nz)) + [0]
    tile = max(min(256, cc), b)
    tiles = cc // tile

    def theirs_at(j):
        return lax.rem(zi + j, nz) * 2 + 1 - par

    def mine_at(j):
        return lax.rem(zi + j, nz) * 2 + par

    places = [theirs_at(j) for j in order] + [mine_at(j) for j in order]

    load_x0 = pltpu.make_async_copy(prhs_hbm.at[0], prhs.at[0], lsem.at[0])
    load_ids = pltpu.make_async_copy(ids_hbm, ids, lsem.at[1])
    load_a = pltpu.make_async_copy(asol_hbm, known.at[pl.ds(mc * ab, ab)], lsem.at[2])
    load_b1 = pltpu.make_async_copy(b_hbm.at[1], vb1, lsem.at[3])
    load_b0 = pltpu.make_async_copy(b_hbm.at[0], vb0.at[pl.ds(0, cap)], lsem.at[4])
    load_d1 = pltpu.make_async_copy(d_hbm.at[1], vd1, lsem.at[5])
    load_x1 = pltpu.make_async_copy(prhs_hbm.at[1], prhs.at[1], lsem.at[6])
    load_r = pltpu.make_async_copy(arhs_hbm, arhs, lsem.at[7])
    load_d0 = [
        pltpu.make_async_copy(rows(d_hbm.at[0], place, b), rows(vd0, place, b), dsem.at[i])
        for i, place in enumerate(places)
    ]

    barrier = pltpu.get_barrier_semaphore()
    peers = [{"row": mine_at(j)} for j in range(1, nz)]
    peers += [{"row": partner}]
    peers += [{"col": lax.rem(mc + d, m)} for d in range(1, m)]
    for peer in peers:
        pl.semaphore_signal(barrier, inc=1, device_id=peer, device_id_type=MESH)
    load_x0.start()
    for load in load_d0:
        load.start()
    load_a.start()
    load_ids.start()

    sum_f0 = [RowSum(part_f0.at[h], hb, xr.at[0, h], zs.at[0, h], zr.at[0, h]) for h in range(2)]
    sum_f1 = [RowSum(part_f1.at[h], hb, xr.at[1, h], zs.at[1, h], zr.at[1, h]) for h in range(2)]
    sum_b0 = [RowSum(part_b0.at[h], hb, xr.at[2, h], zs.at[2, h], zr.at[2, h]) for h in range(2)]
    sum_b1 = RowSum(part_b1, b, xr1, zs1, zr1)
    gather_f0 = [RowGather(full_f0.at[h], hb) for h in range(2)]
    gather_b1 = [RowGather(full_b1.at[h], hb) for h in range(2)]
    gather_b0 = [RowGather(full_b0.at[h], hb) for h in range(2)]
    gather_f1 = RowGather(full_f1, b)
    col_p = [
        ColReduce(part_p.at[h], full_p.at[h], cl.at[0, h], ys.at[0, h], yl.at[0, h])
        for h in range(2)
    ]
    col_s1 = [
        ColReduce(part_s1.at[h], full_s1.at[h], cl.at[1, h], ys.at[1, h], yl.at[1, h])
        for h in range(2)
    ]
    sum_s0 = [ColSum(part_s0.at[h], cr.at[h], hq) for h in range(2)]
    sum_u = ColSum(part_u, cru, a)
    gather_a = ColGather(known, ab)

    def first(i):
        load_d0[i].wait()
        place = places[i]
        value = jnp.dot(get(vd0, place, b), x0, preferred_element_type=F32)
        for h in range(2):
            put(part_f0.at[h], place, hb, pack(part_of(value, h), b).astype(BF))

    load_x0.wait()
    x0 = prhs[0]
    for i in range(2 * nz):
        first(i)
    for load in (load_b1, load_b0, load_d1, load_x1, load_r):
        load.start()
    def find(which, start, count, base):
        def step(k, carry):
            slot = jnp.int32(cap)
            for s in range(cap):
                slot = jnp.where(ids[which, s] == start + k, s, slot)
            idx[base + k] = slot
            return carry

        lax.fori_loop(0, count, step, 0)

    def prepare():
        known_t[na] = jnp.zeros((nrhs, bs), BF)
        vb0[cap] = jnp.zeros((bs, cc), BF)
        slots[0, cap] = jnp.zeros((bs, nrhs), F32)
        slots[1, cap] = jnp.zeros((bs, nrhs), F32)
        load_ids.wait()
        find(0, me * pb, pb, o_pan)
        for which, base in ((0, o_p0), (1, o_p1)):
            for s in range(cap):
                position = ids[which, s] - z["pw"] - me * na
                inside = jnp.logical_and(position >= 0, position < na)
                idx[base + s] = jnp.where(inside, position, na)

    def find_later(which):
        find(which, z["pw"] + me * na, na, (o_l0, o_l1)[which])

    def turn(side):
        def step(i, carry):
            at = ((i // ab) * 2 + side) * ab + i % ab
            known_t[at] = known[at].astype(F32).T.astype(BF)
            return carry

        lax.fori_loop(0, na // 2, step, 0)

    def gather_values(which, offset):
        for s in range(cap):
            vt[which, :, s * bs:(s + 1) * bs] = known_t[idx[offset + s]]

    def back_tile(which, vb, t):
        cols = span(t, tile)
        return jnp.dot(
            vt[which], vb[0:cap, :, cols].reshape(cap * bs, tile),
            preferred_element_type=F32,
        )

    def one_tiles(lo, hi):
        def step(t, carry):
            put(part_b1, t, tile, back_tile(1, vb1, t).T.astype(BF))
            return carry

        lax.fori_loop(lo, hi, step, 0)

    def zero_tiles(lo, hi):
        def step(t, carry):
            acc_t[:, span(t, tile)] = back_tile(0, vb0, t)
            return carry

        lax.fori_loop(lo, hi, step, 0)

    group = 2 if cap % 2 == 0 else 1
    groups = cap // group

    def later(which, vb, lo, hi):
        def step(t, carry):
            block = vb[pl.ds(t * group, group)].reshape(group * bs, cc)
            value = jnp.dot(block, wide[which], preferred_element_type=F32)
            slots[which, pl.ds(t * group, group)] = value.reshape(group, bs, nrhs)
            return carry

        lax.fori_loop(lo, hi, step, 0)

    fine_rows = b % 128 == 0
    fine_cols = q % 128 == 0
    steps_p = max(1, min(2, pb // 2))
    halves_p = (pb // 2) // steps_p

    def blocks_of(ref, at, size):
        return jnp.concatenate([get(ref, at(j), size) for j in range(nz)], axis=0)

    def panel_slots(half, t, at):
        found = []
        for i in range(steps_p):
            slot = idx[o_pan + half * (pb // 2) + t * steps_p + i]
            if at is None:
                found.append(vb0[slot])
            else:
                found.append(jnp.concatenate(
                    [vb0[slot, :, span(at(j), b)] for j in range(nz)], axis=1
                ))
        return jnp.concatenate(found, axis=0)

    tile_p = steps_p * bs

    def panel_first(h):
        x = unpack(blocks_of(full_f0.at[h], mine_at, hb), b).astype(BF)
        for half in range(2):
            for t in range(halves_p):
                value = jnp.dot(panel_slots(half, t, mine_at), x, preferred_element_type=F32)
                acc_p[h, pl.ds((half * halves_p + t) * tile_p, tile_p), :] = value

    def panel_rest(h):
        if fine_rows:
            x = unpack(blocks_of(full_f0.at[h], theirs_at, hb), b).astype(BF)
        else:
            x = unpack(full_f0[h], b).astype(BF)

        def one(half, t):
            value = jnp.dot(
                panel_slots(half, t, theirs_at if fine_rows else None), x,
                preferred_element_type=F32,
            )
            if fine_rows:
                value = value + acc_p[h, span(half * halves_p + t, tile_p), :]
            return pack(value, q)

        red = col_p[h]
        for t in range(halves_p):
            put(part_p.at[h], (1 - core) * halves_p + t, tile_p // 2, one(1 - core, t).astype(BF))
        red.send_twin()
        red.send_y(jnp.concatenate([one(core, t) for t in range(halves_p)], axis=0))

    def solve_forward(h):
        cols = [span(core, p // 2), span(1 - core, p // 2)]
        x = unpack(get(full_p.at[h], core, hp), q).astype(BF)
        for place in places:
            value = jnp.dot(vd1[span(place, b), cols[0]], x, preferred_element_type=F32)
            acc_f[h, span(place, b), :] = value
        if h == 0:
            sum_b1.forward()
        col_p[h].finish()
        x = unpack(get(full_p.at[h], 1 - core, hp), q).astype(BF)
        for i, place in enumerate(places):
            value = jnp.dot(vd1[span(place, b), cols[1]], x, preferred_element_type=F32)
            value = value + acc_f[h, span(place, b), :]
            put(part_f1.at[h], place, hb, pack(value, b).astype(BF))
            if i < nz:
                sum_f1[h].send_x(order[i])

    def back_first(h, full, vd):
        xt = unpack(blocks_of(full.at[h], mine_at, hb), b).T.astype(BF)
        acc_s[h] = jnp.dot(xt, blocks_of(vd, mine_at, b), preferred_element_type=F32)

    def back_input(h, full):
        return unpack(blocks_of(full.at[h], theirs_at, hb), b).T.astype(BF)

    def back_columns(h, xt, vd, cols):
        block = jnp.concatenate([vd[span(theirs_at(j), b), cols] for j in range(nz)], axis=0)
        yt = acc_s[h, :, cols] + jnp.dot(xt, block, preferred_element_type=F32)
        return pack(yt.T, q)

    def solve_back_one(h):
        xt = back_input(h, full_b1)
        red = col_s1[h]
        put(part_s1.at[h], 1 - core, hp,
            back_columns(h, xt, vd1, span(1 - core, p // 2)).astype(BF))
        red.send_twin()
        red.send_y(back_columns(h, xt, vd1, span(core, p // 2)))

    def solve_back_zero(h):
        xt = back_input(h, full_b0)
        dests = sorted(range(1, m), key=lambda d: d % 2) + [0]
        if fine_cols:
            for d in dests:
                place = lax.rem(mc + d, m)
                put(part_s0.at[h], place, hq,
                    back_columns(h, xt, vd0, span(place, q)).astype(BF))
                if d:
                    sum_s0[h].send_to(d)
        else:
            part_s0[h] = back_columns(h, xt, vd0, pl.ds(0, p)).astype(BF)
            for d in range(1, m):
                sum_s0[h].send_to(d)

    def panel_columns(half, cols):
        return jnp.concatenate(
            [vb0[idx[o_pan + half * (pb // 2) + i], :, cols] for i in range(pb // 2)], axis=0
        )

    def panel_back(h):
        lanes = slice(h * hn, (h + 1) * hn)
        fine = tile == b
        order_t = places if fine else list(range(tiles))
        st = unpack(get(full_s1.at[h], core, hp), q).T.astype(BF)
        for t in order_t:
            cols = span(t, tile)
            value = jnp.dot(st, panel_columns(core, cols), preferred_element_type=F32)
            acc_t[lanes, cols] = acc_t[lanes, cols] + value
        col_s1[h].finish()
        st = unpack(get(full_s1.at[h], 1 - core, hp), q).T.astype(BF)
        for i, t in enumerate(order_t):
            cols = span(t, tile)
            value = jnp.dot(st, panel_columns(1 - core, cols), preferred_element_type=F32)
            value = (value + acc_t[lanes, cols]).T
            put(part_b0.at[h], t, tile // 2, pack(value, b).astype(BF))
            if fine and i < nz:
                sum_b0[h].send_x(order[i])
        if not fine:
            for j in order:
                sum_b0[h].send_x(j)

    def chain(h):
        sum_f0[h].forward()
        yield
        put(full_f0.at[h], me, hb, sum_f0[h].finish().astype(BF))
        gather_f0[h].start()
        yield
        gather_f0[h].forward()
        if fine_rows:
            if h == 0:
                load_b0.wait()
            panel_first(h)
        yield
        gather_f0[h].finish()
        if h == 0 and not fine_rows:
            load_b0.wait()
        panel_rest(h)
        yield
        mine = pack(part_of(prhs[1, span(core, p // 2), :].astype(F32), h), q)
        col_p[h].share((mine - col_p[h].total()).astype(BF))
        solve_forward(h)
        yield
        sum_f1[h].forward()
        yield
        f1_mine = sum_f1[h].finish().astype(BF)
        put(full_b1.at[h], me, hb, (f1_mine.astype(F32) - b1_mine[h]).astype(BF))
        gather_b1[h].start()
        put(full_f1, me * 2 + h, hb, f1_mine)
        yield
        gather_b1[h].forward()
        back_first(h, full_b1, vd1)
        yield
        gather_b1[h].finish()
        solve_back_one(h)
        yield
        col_s1[h].share(col_s1[h].total().astype(BF))
        panel_back(h)
        yield
        sum_b0[h].forward()
        yield
        b0_mine = sum_b0[h].finish()
        f0_mine = get(full_f0.at[h], me, hb).astype(F32)
        put(full_b0.at[h], me, hb, (f0_mine - b0_mine).astype(BF))
        gather_b0[h].start()
        yield
        gather_b0[h].forward()
        back_first(h, full_b0, vd0)
        yield
        gather_b0[h].finish()
        solve_back_zero(h)
        yield

    def widen(which, full):
        if which == 0:
            parts = [full_f0[h] for h in range(2)]
        else:
            blocks = full_f1[...].reshape(n, 2, hb, nrhs)
            parts = [blocks[:, h].reshape(n * hb, nrhs) for h in range(2)]
        wide[which] = jnp.concatenate([unpack(v, b).astype(BF) for v in parts], axis=1)

    def send_b1():
        for j in order:
            sum_b1.send_x(j)

    def finish_b1():
        total = sum_b1.finish()
        for h in range(2):
            b1_mine[h] = pack(part_of(total, h), b)

    def begin_one():
        gather_f1.finish()
        widen(1, full_f1)

    def add_update():
        for k in range(na):
            value = slots[0, idx[o_l0 + k]] + slots[1, idx[o_l1 + k]]
            part_u[k * bs:(k + 1) * bs, :] = value.astype(BF)
        for d in range(1, m):
            sum_u.send_to(d)

    def save_one():
        halves = [unpack(get(full_s1.at[h], mc, hq), q).astype(BF) for h in range(2)]
        sol[1] = jnp.concatenate(halves, axis=1)
        save_s1.start()

    def finish_update():
        load_r.wait()
        upd[...] = (arhs[...].astype(F32) - sum_u.finish()).astype(BF)
        save_u.start()

    save_s1 = pltpu.make_async_copy(sol.at[1], sol_hbm.at[1], osem.at[0])
    save_s0 = pltpu.make_async_copy(sol.at[0], sol_hbm.at[0], osem.at[1])
    save_u = pltpu.make_async_copy(upd, upd_hbm, osem.at[2])

    call = functools.partial

    def piece(work, total, lo, hi, parts=8):
        return call(work, lo * total // parts, hi * total // parts)

    ones, zeros = call(piece, one_tiles, tiles), call(piece, zero_tiles, tiles)
    later_0 = call(piece, call(later, 0, vb0), groups)
    later_1 = call(piece, call(later, 1, vb1), groups)
    side = {
        (0, 1): [gather_a.forward, call(turn, core)],
        (1, 0): [gather_a.finish, call(turn, 1 - core), call(gather_values, 1, o_p1)],
        (1, 1): [load_b1.wait, ones(0, 4)],
        (2, 0): [ones(4, 6)],
        (2, 1): [ones(6, 8), send_b1],
        (3, 0): [call(gather_values, 0, o_p0)],
        (3, 1): [call(widen, 0, None), later_0(0, 1), load_d1.wait, load_x1.wait],
        (4, 0): [later_0(1, 3)],
        (4, 1): [later_0(3, 6)],
        (5, 0): [later_0(6, 8)],
        (5, 1): [finish_b1, zeros(0, 1)],
        (6, 0): [zeros(1, 3)],
        (6, 1): [zeros(3, 5)],
        (7, 0): [gather_f1.start, zeros(5, 6)],
        (7, 1): [zeros(6, 7)],
        (8, 0): [zeros(7, 8)],
        (8, 1): [gather_f1.forward],
        (9, 1): [save_one],
        (10, 0): [begin_one, later_1(0, 1)],
        (10, 1): [later_1(1, 4)],
        (11, 0): [later_1(4, 6)],
        (11, 1): [later_1(6, 8), add_update],
        (13, 1): [finish_update],
    }
    prepare()
    pl.semaphore_wait(barrier, len(peers))
    for j in order:
        sum_f0[0].send_x(j)
    load_a.wait()
    gather_a.start()
    for j in order:
        sum_f0[1].send_x(j)
    find_later(0)
    find_later(1)
    chains = [chain(0), chain(1)]
    sent = []
    for it in range(14):
        for h in range(2):
            next(chains[h])
            for task in side.get((it, h), ()):
                task()
        sent.append(len(pending))
        if it >= 2:
            count = sent[it - 2]
            settle(count)
            sent = [s - count for s in sent]

    halves = [unpack(sum_s0[h].finish(), q).astype(BF) for h in range(2)]
    sol[0] = jnp.concatenate(halves, axis=1)
    save_s0.start()
    settle(len(pending))
    save_s1.wait()
    save_u.wait()
    save_s0.wait()


def hand_over(sol, upd, sol_out, upd_out):
    sol_out[...] = sol[...]
    upd_out[...] = upd[...]


def on_device(diag, panel_rhs, below, row_ids, ancestor_rhs, ancestor_solution):
    n, m = lax.axis_size("row"), lax.axis_size("col")
    z = sizes_of(n, m, diag, panel_rhs, below, row_ids, ancestor_rhs)
    nz, b, q = z["nz"], z["b"], z["q"]
    cc, p, cap, bs, nrhs, na, pb = (z[k] for k in ("cc", "p", "cap", "bs", "nrhs", "na", "pb"))
    a, ab, hn, ny = z["a"], z["ab"], z["nrhs"] // 2, m // 2

    hbm = pl.BlockSpec(memory_space=pl.ANY)
    nsem = 14 * 2 * nz + 4 * (2 + ny) + 4 * m + 2 * ny
    V = pltpu.VMEM
    shapes = (
        jax.ShapeDtypeStruct((2, q, nrhs), BF),
        jax.ShapeDtypeStruct((a, nrhs), BF),
    )
    made = pl.pallas_call(
        functools.partial(kernel, z),
        out_shape=shapes,
        in_specs=[hbm] * 6,
        out_specs=(hbm, hbm),
        scratch_shapes=[
            pltpu.SMEM((2, cap), jnp.int32), pltpu.SMEM((pb + 2 * na + 2 * cap,), jnp.int32),
            V((cc, p), BF), V((cc, p), BF),
            V((cap + 1, bs, cc), BF), V((cap, bs, cc), BF),
            V((2, p, nrhs), BF), V((a, nrhs), BF), V((2, q, nrhs), BF), V((a, nrhs), BF),
            V((na, bs, nrhs), BF), V((na + 1, nrhs, bs), BF), V((2, nrhs, cap * bs), BF),
            V((2, cap + 1, bs, nrhs), F32), V((nrhs, cc), F32),
            V((2, p, hn), F32), V((2, cc, hn), F32), V((2, hn, p), F32), V((2, b // 2, nrhs), F32),
            V((cc, nrhs), BF), V((cc, nrhs), BF), V((2, cc, nrhs), BF),
        ] + [V((2, cc // 2, nrhs), BF)] * 6 + [V((3, 2, nz, b // 2, nrhs), BF)] * 3 + [
            V((nz, b, nrhs), BF)
        ] * 3 + [V((2, p // 2, nrhs), BF)] * 5 + [
            V((na * bs, nrhs), BF),
            V((2, 2, p // 4, nrhs), BF), V((2, 2, p // 4, nrhs), BF),
            V((2, 2, ny, p // 4, nrhs), BF),
            V((2, m, q // 2, nrhs), BF), V((m, a, nrhs), BF),
            pltpu.SemaphoreType.DMA((8,)),
            pltpu.SemaphoreType.DMA((n,)),
            pltpu.SemaphoreType.DMA((3,)),
            pltpu.SemaphoreType.DMA((nsem,)),
            pltpu.SemaphoreType.DMA((nsem,)),
        ],
        compiler_params=pltpu.CompilerParams(
            collective_id=0, has_side_effects=True, vmem_limit_bytes=62 * 1024 * 1024
        ),
    )(
        row_ids, diag, panel_rhs, below.reshape(2, cap, bs, cc), ancestor_rhs,
        ancestor_solution.reshape(ab, bs, nrhs),
    )
    vmem = pl.BlockSpec(memory_space=pltpu.VMEM)
    return pl.pallas_call(
        hand_over,
        out_shape=shapes,
        in_specs=[vmem] * 2,
        out_specs=(vmem, vmem),
    )(*made)


def solution(mesh):
    in_specs = (
        P(None, "col", "row"),
        P(None, "row", None),
        P(None, "row", "col"),
        P(None, "row"),
        P(("row", "col"), None),
        P(("row", "col"), None),
    )
    out_specs = (P(None, ("row", "col"), None), P(("row", "col"), None))
    return jax.shard_map(
        on_device, mesh=mesh, in_specs=in_specs, out_specs=out_specs, check_vma=False
    )
```

```python
import functools

import jax
import jax.numpy as jnp
from jax import lax
from jax.experimental import pallas as pl
from jax.experimental.pallas import tpu as pltpu
from jax.sharding import PartitionSpec as P

MESH = pl.DeviceIdType.MESH
BF = jnp.bfloat16
F32 = jnp.float32


def sizes_of(n, m, diag, panel_rhs, below, row_ids, ancestor_rhs):
    z = {}
    z["n"], z["m"] = n, m
    z["nz"] = n // 2
    z["cc"], z["p"] = diag.shape[1], diag.shape[2]
    z["nrhs"] = panel_rhs.shape[2]
    z["cap"] = row_ids.shape[1]
    z["bs"] = below.shape[1] // z["cap"]
    z["b"] = z["cc"] // n
    z["q"] = z["p"] // m
    z["a"] = ancestor_rhs.shape[0]
    z["ab"] = z["a"] // z["bs"]
    z["na"] = z["ab"] * m
    z["pb"] = z["p"] // z["bs"]
    z["pw"] = z["cc"] * m // z["bs"]
    return z


def kernel(
    z, ids_hbm, d_hbm, prhs_hbm, b_hbm, arhs_hbm, asol_hbm, sol_hbm, upd_hbm,
    ids, idx, vd0, vd1, vb0, vb1, prhs, arhs, sol, upd, known, known_t, vt, slots, acc_t,
    acc_p, acc_f, acc_s, b1_mine,
    part_b1, full_f1, wide, part_f0, part_f1, part_b0, full_f0, full_b1, full_b0,
    xr, zs, zr, xr1, zs1, zr1, part_p, full_p, part_s1, full_s1, part_s0, part_u,
    cl, ys, yl, cr, cru,
    lsem, dsem, osem, ssem, rsem,
):
    n, m, nz, b, q = z["n"], z["m"], z["nz"], z["b"], z["q"]
    cc, cap, bs, nrhs, na, pb = z["cc"], z["cap"], z["bs"], z["nrhs"], z["na"], z["pb"]
    ab, a, p = z["ab"], z["a"], z["p"]
    me = lax.axis_index("row")
    mc = lax.axis_index("col")
    par = lax.rem(me, 2)
    zi = me // 2
    partner = me + 1 - 2 * par
    core = lax.rem(mc, 2)
    yi = mc // 2
    ny = m // 2
    twin = mc + 1 - 2 * core
    o_pan, o_l0, o_l1, o_p0, o_p1 = 0, pb, pb + na, pb + 2 * na, pb + 2 * na + cap

    paired = nz & (nz - 1) == 0

    def across(j, back=False):
        if not paired:
            return lax.rem(zi + (nz - j if back else j), nz)
        place, bit = zi, 1
        while bit < nz:
            if j & bit:
                place = place + bit * (1 - 2 * lax.rem(zi // bit, 2))
            bit *= 2
        return place

    counter = [0]
    pending = []

    def send(src, dst, axis, place, slot):
        cp = pltpu.make_async_remote_copy(
            src_ref=src, dst_ref=dst, send_sem=ssem.at[slot], recv_sem=rsem.at[slot],
            device_id={axis: place}, device_id_type=MESH,
        )
        cp.start()
        pending.append(cp)
        return cp

    def settle(count):
        for cp in pending[:count]:
            cp.wait_send()
        del pending[:count]

    def take(count):
        base = counter[0]
        counter[0] += count
        return base

    def span(block, size):
        return pl.ds(pl.multiple_of(block * size, size), size)

    def rows(ref, block, size):
        return ref.at[span(block, size)]

    def get(ref, block, size):
        return ref[span(block, size), :]

    def put(ref, block, size, value):
        ref[span(block, size), :] = value

    class RowSum:
        def __init__(self, part, size, xr, zs, zr):
            self.part, self.size = part, size
            self.xr, self.zs, self.zr = xr, zs, zr
            self.xk, self.zk = take(nz), take(nz)
            self.xc, self.zc = {}, {}

        def send_x(self, j):
            zd = across(j)
            self.xc[j] = send(
                rows(self.part, zd * 2 + 1 - par, self.size), self.xr.at[j], "row", partner,
                self.xk + j,
            )

        def forward(self):
            for j in order[:-1]:
                zd = across(j)
                self.xc[j].wait_recv()
                mine = get(self.part, zd * 2 + par, self.size)
                self.zs[j] = (mine.astype(F32) + self.xr[j].astype(F32)).astype(BF)
                self.zc[j] = send(
                    self.zs.at[j], self.zr.at[j], "row", zd * 2 + par, self.zk + j
                )

        def finish(self):
            self.xc[0].wait_recv()
            total = get(self.part, me, self.size).astype(F32) + self.xr[0].astype(F32)
            for j in order[:-1]:
                self.zc[j].wait_recv()
                total = total + self.zr[j].astype(F32)
            return total

    class RowGather:
        def __init__(self, full, size):
            self.full, self.size = full, size
            self.xk, self.zk = take(nz), take(nz)
            self.xc, self.zc = {}, {}

        def start(self):
            mine = rows(self.full, me, self.size)
            for j in order[:-1]:
                self.zc[j] = send(mine, mine, "row", across(j) * 2 + par, self.zk + j)
            self.xc[0] = send(mine, mine, "row", partner, self.xk)

        def forward(self):
            for j in order[:-1]:
                self.zc[j].wait_recv()
                theirs = rows(self.full, across(j, True) * 2 + par, self.size)
                self.xc[j] = send(theirs, theirs, "row", partner, self.xk + j)

        def finish(self):
            for j in range(nz):
                self.xc[j].wait_recv()

    class ColSum:
        def __init__(self, part, landing, size):
            self.part, self.landing, self.size = part, landing, size
            self.s = take(m)
            self.c = {}

        def send_to(self, d):
            place = lax.rem(mc + d, m)
            self.c[d] = send(
                rows(self.part, place, self.size), self.landing.at[d], "col", place, self.s + d
            )

        def finish(self):
            total = get(self.part, mc, self.size).astype(F32)
            for d in range(1, m):
                self.c[d].wait_recv()
                total = total + self.landing[d].astype(F32)
            return total

    class ColGather:
        def __init__(self, full, size):
            self.full, self.size = full, size
            self.s, self.t = take(ny), take(ny)
            self.y, self.c = {}, {}

        def start(self):
            mine = rows(self.full, mc, self.size)
            for d in range(1, ny):
                place = lax.rem(yi + d, ny) * 2 + core
                self.y[d] = send(mine, mine, "col", place, self.s + d)
            self.c[0] = send(mine, mine, "col", twin, self.t)

        def forward(self):
            for d in range(1, ny):
                self.y[d].wait_recv()
                theirs = rows(self.full, lax.rem(yi + ny - d, ny) * 2 + core, self.size)
                self.c[d] = send(theirs, theirs, "col", twin, self.t + d)

        def finish(self):
            for d in range(ny):
                self.c[d].wait_recv()

    hp = p // 4

    class ColReduce:
        def __init__(self, part, full, twin_in, out, landing):
            self.part, self.full, self.twin_in = part, full, twin_in
            self.out, self.landing = out, landing
            self.s = take(2 + ny)
            self.c = {}

        def send_twin(self):
            self.t = send(
                rows(self.part, 1 - core, hp), self.twin_in, "col", twin, self.s
            )

        def send_y(self, mine):
            self.t.wait_recv()
            self.out[...] = (mine + self.twin_in[...].astype(F32)).astype(BF)
            for d in range(1, ny):
                place = lax.rem(yi + d, ny) * 2 + core
                self.c[d] = send(self.out, self.landing.at[d], "col", place, self.s + 1 + d)

        def total(self):
            total = self.out[...].astype(F32)
            for d in range(1, ny):
                self.c[d].wait_recv()
                total = total + self.landing[d].astype(F32)
            return total

        def share(self, value):
            put(self.full, core, hp, value)
            mine = rows(self.full, core, hp)
            self.g = send(mine, mine, "col", twin, self.s + 1)

        def finish(self):
            self.g.wait_recv()

    hb, hq, hn = b // 2, q // 2, nrhs // 2

    def pack(value, size):
        blocks = value.reshape(-1, size, hn)
        half = size // 2
        both = jnp.concatenate([blocks[:, :half], blocks[:, half:]], axis=2)
        return both.reshape(-1, nrhs)

    def unpack(value, size):
        half = size // 2
        blocks = value.astype(F32).reshape(-1, half, nrhs)
        both = jnp.concatenate([blocks[:, :, :hn], blocks[:, :, hn:]], axis=1)
        return both.reshape(-1, hn)

    def both_of(v0, v1, size):
        half = size // 2
        p0, p1 = (v.astype(F32).reshape(-1, half, nrhs) for v in (v0, v1))
        top = jnp.concatenate([p0[:, :, :hn], p1[:, :, :hn]], axis=2)
        low = jnp.concatenate([p0[:, :, hn:], p1[:, :, hn:]], axis=2)
        return jnp.concatenate([top, low], axis=1).reshape(-1, nrhs)

    def part_of(value, h):
        return value[:, h * hn:(h + 1) * hn]

    order = list(range(nz - 1, -1, -1))
    tile = max(min(256, cc), b)
    tiles = cc // tile

    def theirs_at(j):
        return across(j) * 2 + 1 - par

    def mine_at(j):
        return across(j) * 2 + par

    places = [theirs_at(j) for j in order] + [mine_at(j) for j in order]

    load_x0 = pltpu.make_async_copy(prhs_hbm.at[0], prhs.at[0], lsem.at[0])
    load_ids = pltpu.make_async_copy(ids_hbm, ids, lsem.at[1])
    load_a = pltpu.make_async_copy(asol_hbm, known.at[pl.ds(mc * ab, ab)], lsem.at[2])
    load_b1 = pltpu.make_async_copy(b_hbm.at[1], vb1, lsem.at[3])
    load_b0 = pltpu.make_async_copy(b_hbm.at[0], vb0.at[pl.ds(0, cap)], lsem.at[4])
    load_d1 = pltpu.make_async_copy(d_hbm.at[1], vd1, lsem.at[5])
    load_x1 = pltpu.make_async_copy(prhs_hbm.at[1], prhs.at[1], lsem.at[6])
    load_r = pltpu.make_async_copy(arhs_hbm, arhs, lsem.at[7])
    load_d0 = [
        pltpu.make_async_copy(rows(d_hbm.at[0], place, b), rows(vd0, place, b), dsem.at[i])
        for i, place in enumerate(places)
    ]

    barrier = pltpu.get_barrier_semaphore()
    peers = [{"row": mine_at(j)} for j in range(1, nz)]
    peers += [{"row": partner}]
    peers += [{"col": lax.rem(mc + d, m)} for d in range(1, m)]
    for peer in peers:
        pl.semaphore_signal(barrier, inc=1, device_id=peer, device_id_type=MESH)
    load_x0.start()
    for load in load_d0:
        load.start()
    load_a.start()
    load_ids.start()

    sum_f0 = [RowSum(part_f0.at[h], hb, xr.at[0, h], zs.at[0, h], zr.at[0, h]) for h in range(2)]
    sum_f1 = [RowSum(part_f1.at[h], hb, xr.at[1, h], zs.at[1, h], zr.at[1, h]) for h in range(2)]
    sum_b0 = [RowSum(part_b0.at[h], hb, xr.at[2, h], zs.at[2, h], zr.at[2, h]) for h in range(2)]
    sum_b1 = RowSum(part_b1, b, xr1, zs1, zr1)
    gather_f0 = [RowGather(full_f0.at[h], hb) for h in range(2)]
    gather_b1 = [RowGather(full_b1.at[h], hb) for h in range(2)]
    gather_b0 = [RowGather(full_b0.at[h], hb) for h in range(2)]
    gather_f1 = RowGather(full_f1, b)
    col_p = [
        ColReduce(part_p.at[h], full_p.at[h], cl.at[0, h], ys.at[0, h], yl.at[0, h])
        for h in range(2)
    ]
    col_s1 = [
        ColReduce(part_s1.at[h], full_s1.at[h], cl.at[1, h], ys.at[1, h], yl.at[1, h])
        for h in range(2)
    ]
    sum_s0 = [ColSum(part_s0.at[h], cr.at[h], hq) for h in range(2)]
    sum_u = ColSum(part_u, cru, a)
    gather_a = ColGather(known, ab)

    def first(i):
        load_d0[i].wait()
        place = places[i]
        value = jnp.dot(get(vd0, place, b), x0, preferred_element_type=F32)
        for h in range(2):
            put(part_f0.at[h], place, hb, pack(part_of(value, h), b).astype(BF))

    load_x0.wait()
    x0 = prhs[0]
    for i in range(nz):
        first(i)
    for load in (load_b1, load_b0, load_d1, load_x1, load_r):
        load.start()
    def find(which, start, count, base):
        def step(k, carry):
            slot = jnp.int32(cap)
            for s in range(cap):
                slot = jnp.where(ids[which, s] == start + k, s, slot)
            idx[base + k] = slot
            return carry

        lax.fori_loop(0, count, step, 0)

    def prepare():
        known_t[na] = jnp.zeros((nrhs, bs), BF)
        vb0[cap] = jnp.zeros((bs, cc), BF)
        slots[0, cap] = jnp.zeros((bs, nrhs), F32)
        slots[1, cap] = jnp.zeros((bs, nrhs), F32)
        load_ids.wait()
        find(0, me * pb, pb, o_pan)
        for which, base in ((0, o_p0), (1, o_p1)):
            for s in range(cap):
                position = ids[which, s] - z["pw"] - me * na
                inside = jnp.logical_and(position >= 0, position < na)
                idx[base + s] = jnp.where(inside, position, na)

    def find_later(which):
        find(which, z["pw"] + me * na, na, (o_l0, o_l1)[which])

    def turn(side):
        def step(i, carry):
            at = ((i // ab) * 2 + side) * ab + i % ab
            known_t[at] = known[at].astype(F32).T.astype(BF)
            return carry

        lax.fori_loop(0, na // 2, step, 0)

    def gather_values(which, offset):
        for s in range(cap):
            vt[which, :, s * bs:(s + 1) * bs] = known_t[idx[offset + s]]

    def back_tile(which, vb, t):
        cols = span(t, tile)
        return jnp.dot(
            vt[which], vb[0:cap, :, cols].reshape(cap * bs, tile),
            preferred_element_type=F32,
        )

    def one_tiles(lo, hi):
        def step(t, carry):
            put(part_b1, t, tile, back_tile(1, vb1, t).T.astype(BF))
            return carry

        lax.fori_loop(lo, hi, step, 0)

    def zero_tiles(lo, hi):
        def step(t, carry):
            acc_t[:, span(t, tile)] = back_tile(0, vb0, t)
            return carry

        lax.fori_loop(lo, hi, step, 0)

    group = 2 if cap % 2 == 0 else 1
    groups = cap // group

    def later(which, vb, lo, hi):
        def step(t, carry):
            block = vb[pl.ds(t * group, group)].reshape(group * bs, cc)
            value = jnp.dot(block, wide[which], preferred_element_type=F32)
            slots[which, pl.ds(t * group, group)] = value.reshape(group, bs, nrhs)
            return carry

        lax.fori_loop(lo, hi, step, 0)

    fine_rows = b % 128 == 0
    fine_cols = q % 128 == 0
    steps_p = max(1, min(2, pb // 2))
    halves_p = (pb // 2) // steps_p

    def blocks_of(ref, at, size):
        return jnp.concatenate([get(ref, at(j), size) for j in range(nz)], axis=0)

    def panel_slots(half, t, at):
        found = []
        for i in range(steps_p):
            slot = idx[o_pan + half * (pb // 2) + t * steps_p + i]
            if at is None:
                found.append(vb0[slot])
            else:
                found.append(jnp.concatenate(
                    [vb0[slot, :, span(at(j), b)] for j in range(nz)], axis=1
                ))
        return jnp.concatenate(found, axis=0)

    tile_p = steps_p * bs

    def panel_first():
        x = both_of(*(blocks_of(full_f0.at[h], mine_at, hb) for h in range(2)), b).astype(BF)
        for half in range(2):
            for t in range(halves_p):
                value = jnp.dot(panel_slots(half, t, mine_at), x, preferred_element_type=F32)
                for h in range(2):
                    at = pl.ds((half * halves_p + t) * tile_p, tile_p)
                    acc_p[h, at, :] = part_of(value, h)

    def panel_rest(h):
        if fine_rows:
            x = unpack(blocks_of(full_f0.at[h], theirs_at, hb), b).astype(BF)
        else:
            x = unpack(full_f0[h], b).astype(BF)

        def one(half, t):
            value = jnp.dot(
                panel_slots(half, t, theirs_at if fine_rows else None), x,
                preferred_element_type=F32,
            )
            if fine_rows:
                value = value + acc_p[h, span(half * halves_p + t, tile_p), :]
            return pack(value, q)

        red = col_p[h]
        for t in range(halves_p):
            put(part_p.at[h], (1 - core) * halves_p + t, tile_p // 2, one(1 - core, t).astype(BF))
        red.send_twin()
        red.send_y(jnp.concatenate([one(core, t) for t in range(halves_p)], axis=0))

    def solve_forward(h):
        cols = [span(core, p // 2), span(1 - core, p // 2)]
        x = unpack(get(full_p.at[h], core, hp), q).astype(BF)
        for place in places:
            value = jnp.dot(vd1[span(place, b), cols[0]], x, preferred_element_type=F32)
            acc_f[h, span(place, b), :] = value
        if h == 0:
            sum_b1.forward()
        col_p[h].finish()
        x = unpack(get(full_p.at[h], 1 - core, hp), q).astype(BF)
        for i, place in enumerate(places):
            value = jnp.dot(vd1[span(place, b), cols[1]], x, preferred_element_type=F32)
            value = value + acc_f[h, span(place, b), :]
            put(part_f1.at[h], place, hb, pack(value, b).astype(BF))
            if i < nz:
                sum_f1[h].send_x(order[i])

    def back_first(full, vd):
        x = both_of(*(blocks_of(full.at[h], mine_at, hb) for h in range(2)), b)
        acc_s[...] = jnp.dot(
            x.T.astype(BF), blocks_of(vd, mine_at, b), preferred_element_type=F32
        )

    def back_input(h, full):
        return unpack(blocks_of(full.at[h], theirs_at, hb), b).T.astype(BF)

    def back_columns(h, xt, vd, cols):
        block = jnp.concatenate([vd[span(theirs_at(j), b), cols] for j in range(nz)], axis=0)
        yt = acc_s[h * hn:(h + 1) * hn, cols] + jnp.dot(xt, block, preferred_element_type=F32)
        return pack(yt.T, q)

    def solve_back_one(h):
        xt = back_input(h, full_b1)
        red = col_s1[h]
        put(part_s1.at[h], 1 - core, hp,
            back_columns(h, xt, vd1, span(1 - core, p // 2)).astype(BF))
        red.send_twin()
        red.send_y(back_columns(h, xt, vd1, span(core, p // 2)))

    def solve_back_zero(h):
        xt = back_input(h, full_b0)
        dests = sorted(range(1, m), key=lambda d: d % 2) + [0]
        if fine_cols:
            for d in dests:
                place = lax.rem(mc + d, m)
                put(part_s0.at[h], place, hq,
                    back_columns(h, xt, vd0, span(place, q)).astype(BF))
                if d:
                    sum_s0[h].send_to(d)
        else:
            part_s0[h] = back_columns(h, xt, vd0, pl.ds(0, p)).astype(BF)
            for d in range(1, m):
                sum_s0[h].send_to(d)

    def panel_columns(half, cols):
        return jnp.concatenate(
            [vb0[idx[o_pan + half * (pb // 2) + i], :, cols] for i in range(pb // 2)], axis=0
        )

    def panel_back(h):
        lanes = slice(h * hn, (h + 1) * hn)
        fine = tile == b
        order_t = places if fine else list(range(tiles))
        st = unpack(get(full_s1.at[h], core, hp), q).T.astype(BF)
        for t in order_t:
            cols = span(t, tile)
            value = jnp.dot(st, panel_columns(core, cols), preferred_element_type=F32)
            acc_t[lanes, cols] = acc_t[lanes, cols] + value
        col_s1[h].finish()
        st = unpack(get(full_s1.at[h], 1 - core, hp), q).T.astype(BF)
        for i, t in enumerate(order_t):
            cols = span(t, tile)
            value = jnp.dot(st, panel_columns(1 - core, cols), preferred_element_type=F32)
            value = (value + acc_t[lanes, cols]).T
            put(part_b0.at[h], t, tile // 2, pack(value, b).astype(BF))
            if fine and i < nz:
                sum_b0[h].send_x(order[i])
        if not fine:
            for j in order:
                sum_b0[h].send_x(j)

    def chain(h):
        sum_f0[h].forward()
        yield
        put(full_f0.at[h], me, hb, sum_f0[h].finish().astype(BF))
        gather_f0[h].start()
        yield
        gather_f0[h].forward()
        if h == 1:
            load_b0.wait()
            if fine_rows:
                panel_first()
        yield
        gather_f0[h].finish()
        panel_rest(h)
        yield
        mine = pack(part_of(prhs[1, span(core, p // 2), :].astype(F32), h), q)
        col_p[h].share((mine - col_p[h].total()).astype(BF))
        solve_forward(h)
        yield
        sum_f1[h].forward()
        yield
        f1_mine = sum_f1[h].finish().astype(BF)
        put(full_b1.at[h], me, hb, (f1_mine.astype(F32) - b1_mine[h]).astype(BF))
        gather_b1[h].start()
        put(full_f1, me * 2 + h, hb, f1_mine)
        yield
        gather_b1[h].forward()
        if h == 1:
            back_first(full_b1, vd1)
        yield
        gather_b1[h].finish()
        solve_back_one(h)
        yield
        col_s1[h].share(col_s1[h].total().astype(BF))
        panel_back(h)
        yield
        sum_b0[h].forward()
        yield
        b0_mine = sum_b0[h].finish()
        f0_mine = get(full_f0.at[h], me, hb).astype(F32)
        put(full_b0.at[h], me, hb, (f0_mine - b0_mine).astype(BF))
        gather_b0[h].start()
        yield
        gather_b0[h].forward()
        if h == 1:
            back_first(full_b0, vd0)
        yield
        gather_b0[h].finish()
        solve_back_zero(h)
        yield

    def widen(which, full):
        if which == 0:
            parts = [full_f0[h] for h in range(2)]
        else:
            blocks = full_f1[...].reshape(n, 2, hb, nrhs)
            parts = [blocks[:, h].reshape(n * hb, nrhs) for h in range(2)]
        wide[which] = both_of(*parts, b).astype(BF)

    def send_b1():
        for j in order:
            sum_b1.send_x(j)

    def finish_b1():
        total = sum_b1.finish()
        for h in range(2):
            b1_mine[h] = pack(part_of(total, h), b)

    def begin_one():
        gather_f1.finish()
        widen(1, full_f1)

    def add_update():
        for k in range(na):
            value = slots[0, idx[o_l0 + k]] + slots[1, idx[o_l1 + k]]
            part_u[k * bs:(k + 1) * bs, :] = value.astype(BF)
        for d in range(1, m):
            sum_u.send_to(d)

    def save_one():
        halves = [unpack(get(full_s1.at[h], mc, hq), q).astype(BF) for h in range(2)]
        sol[1] = jnp.concatenate(halves, axis=1)
        save_s1.start()

    def finish_update():
        load_r.wait()
        upd[...] = (arhs[...].astype(F32) - sum_u.finish()).astype(BF)
        save_u.start()

    save_s1 = pltpu.make_async_copy(sol.at[1], sol_hbm.at[1], osem.at[0])
    save_s0 = pltpu.make_async_copy(sol.at[0], sol_hbm.at[0], osem.at[1])
    save_u = pltpu.make_async_copy(upd, upd_hbm, osem.at[2])

    call = functools.partial

    def piece(work, total, lo, hi, parts=8):
        return call(work, lo * total // parts, hi * total // parts)

    ones, zeros = call(piece, one_tiles, tiles), call(piece, zero_tiles, tiles)
    later_0 = call(piece, call(later, 0, vb0), groups)
    later_1 = call(piece, call(later, 1, vb1), groups)
    side = {
        (0, 1): [gather_a.forward, call(turn, core)],
        (1, 0): [gather_a.finish, call(turn, 1 - core), call(gather_values, 1, o_p1)],
        (1, 1): [load_b1.wait, ones(0, 4)],
        (2, 0): [ones(4, 6)],
        (2, 1): [ones(6, 8), send_b1],
        (3, 0): [call(gather_values, 0, o_p0)],
        (3, 1): [call(widen, 0, None), later_0(0, 1), load_d1.wait, load_x1.wait],
        (4, 0): [later_0(1, 3)],
        (4, 1): [later_0(3, 6)],
        (5, 0): [later_0(6, 8)],
        (5, 1): [finish_b1, zeros(0, 1)],
        (6, 0): [zeros(1, 3)],
        (6, 1): [zeros(3, 5)],
        (7, 0): [gather_f1.start, zeros(5, 6)],
        (7, 1): [zeros(6, 7)],
        (8, 0): [zeros(7, 8)],
        (8, 1): [gather_f1.forward],
        (9, 1): [save_one],
        (10, 0): [begin_one, later_1(0, 1)],
        (10, 1): [later_1(1, 4)],
        (11, 0): [later_1(4, 6)],
        (11, 1): [later_1(6, 8), add_update],
        (13, 1): [finish_update],
    }
    pl.semaphore_wait(barrier, len(peers))
    for h in range(2):
        for j in order[:-1]:
            sum_f0[h].send_x(j)
    load_a.wait()
    gather_a.start()
    for h in range(2):
        sum_f0[h].send_x(0)
    for i in range(nz, 2 * nz):
        first(i)
    prepare()
    find_later(0)
    find_later(1)
    chains = [chain(0), chain(1)]
    sent = []
    for it in range(14):
        for h in range(2):
            next(chains[h])
            for task in side.get((it, h), ()):
                task()
        sent.append(len(pending))
        if it >= 2:
            count = sent[it - 2]
            settle(count)
            sent = [s - count for s in sent]

    halves = [unpack(sum_s0[h].finish(), q).astype(BF) for h in range(2)]
    sol[0] = jnp.concatenate(halves, axis=1)
    save_s0.start()
    settle(len(pending))
    save_s1.wait()
    save_u.wait()
    save_s0.wait()


def hand_over(sol, upd, sol_out, upd_out):
    sol_out[...] = sol[...]
    upd_out[...] = upd[...]


def on_device(diag, panel_rhs, below, row_ids, ancestor_rhs, ancestor_solution):
    n, m = lax.axis_size("row"), lax.axis_size("col")
    z = sizes_of(n, m, diag, panel_rhs, below, row_ids, ancestor_rhs)
    nz, b, q = z["nz"], z["b"], z["q"]
    cc, p, cap, bs, nrhs, na, pb = (z[k] for k in ("cc", "p", "cap", "bs", "nrhs", "na", "pb"))
    a, ab, hn, ny = z["a"], z["ab"], z["nrhs"] // 2, m // 2

    hbm = pl.BlockSpec(memory_space=pl.ANY)
    nsem = 14 * 2 * nz + 4 * (2 + ny) + 4 * m + 2 * ny
    V = pltpu.VMEM
    shapes = (
        jax.ShapeDtypeStruct((2, q, nrhs), BF),
        jax.ShapeDtypeStruct((a, nrhs), BF),
    )
    made = pl.pallas_call(
        functools.partial(kernel, z),
        out_shape=shapes,
        in_specs=[hbm] * 6,
        out_specs=(hbm, hbm),
        scratch_shapes=[
            pltpu.SMEM((2, cap), jnp.int32), pltpu.SMEM((pb + 2 * na + 2 * cap,), jnp.int32),
            V((cc, p), BF), V((cc, p), BF),
            V((cap + 1, bs, cc), BF), V((cap, bs, cc), BF),
            V((2, p, nrhs), BF), V((a, nrhs), BF), V((2, q, nrhs), BF), V((a, nrhs), BF),
            V((na, bs, nrhs), BF), V((na + 1, nrhs, bs), BF), V((2, nrhs, cap * bs), BF),
            V((2, cap + 1, bs, nrhs), F32), V((nrhs, cc), F32),
            V((2, p, hn), F32), V((2, cc, hn), F32), V((nrhs, p), F32), V((2, b // 2, nrhs), F32),
            V((cc, nrhs), BF), V((cc, nrhs), BF), V((2, cc, nrhs), BF),
        ] + [V((2, cc // 2, nrhs), BF)] * 6 + [V((3, 2, nz, b // 2, nrhs), BF)] * 3 + [
            V((nz, b, nrhs), BF)
        ] * 3 + [V((2, p // 2, nrhs), BF)] * 5 + [
            V((na * bs, nrhs), BF),
            V((2, 2, p // 4, nrhs), BF), V((2, 2, p // 4, nrhs), BF),
            V((2, 2, ny, p // 4, nrhs), BF),
            V((2, m, q // 2, nrhs), BF), V((m, a, nrhs), BF),
            pltpu.SemaphoreType.DMA((8,)),
            pltpu.SemaphoreType.DMA((n,)),
            pltpu.SemaphoreType.DMA((3,)),
            pltpu.SemaphoreType.DMA((nsem,)),
            pltpu.SemaphoreType.DMA((nsem,)),
        ],
        compiler_params=pltpu.CompilerParams(
            collective_id=0, has_side_effects=True, vmem_limit_bytes=62 * 1024 * 1024
        ),
    )(
        row_ids, diag, panel_rhs, below.reshape(2, cap, bs, cc), ancestor_rhs,
        ancestor_solution.reshape(ab, bs, nrhs),
    )
    vmem = pl.BlockSpec(memory_space=pltpu.VMEM)
    return pl.pallas_call(
        hand_over,
        out_shape=shapes,
        in_specs=[vmem] * 2,
        out_specs=(vmem, vmem),
    )(*made)


def solution(mesh):
    in_specs = (
        P(None, "col", "row"),
        P(None, "row", None),
        P(None, "row", "col"),
        P(None, "row"),
        P(("row", "col"), None),
        P(("row", "col"), None),
    )
    out_specs = (P(None, ("row", "col"), None), P(("row", "col"), None))
    return jax.shard_map(
        on_device, mesh=mesh, in_specs=in_specs, out_specs=out_specs, check_vma=False
    )
```

```python
import functools

import jax
import jax.numpy as jnp
from jax import lax
from jax.experimental import pallas as pl
from jax.experimental.pallas import tpu as pltpu
from jax.sharding import PartitionSpec as P

MESH = pl.DeviceIdType.MESH
BF = jnp.bfloat16
F32 = jnp.float32


def sizes_of(n, m, diag, panel_rhs, below, row_ids, ancestor_rhs):
    z = {}
    z["n"], z["m"] = n, m
    z["nz"] = n // 2
    z["cc"], z["p"] = diag.shape[1], diag.shape[2]
    z["nrhs"] = panel_rhs.shape[2]
    z["cap"] = row_ids.shape[1]
    z["bs"] = below.shape[1] // z["cap"]
    z["b"] = z["cc"] // n
    z["q"] = z["p"] // m
    z["a"] = ancestor_rhs.shape[0]
    z["ab"] = z["a"] // z["bs"]
    z["na"] = z["ab"] * m
    z["pb"] = z["p"] // z["bs"]
    z["pw"] = z["cc"] * m // z["bs"]
    return z


def kernel(
    z, ids_hbm, d_hbm, prhs_hbm, b_hbm, arhs_hbm, asol_hbm, sol_hbm, upd_hbm,
    ids, idx, vd0, vd1, vb0, vb1, prhs, arhs, sol, upd, known, known_t, vt, slots, acc_t,
    acc_p, acc_f, acc_s, b1_mine,
    part_b1, full_f1, wide, part_f0, part_f1, part_b0, full_f0, full_b1, full_b0,
    xr, zs, zr, xr1, zs1, zr1, part_p, full_p, part_s1, full_s1, part_s0, part_u,
    cl, ys, yl, cr, cru,
    lsem, dsem, osem, ssem, rsem,
):
    n, m, nz, b, q = z["n"], z["m"], z["nz"], z["b"], z["q"]
    cc, cap, bs, nrhs, na, pb = z["cc"], z["cap"], z["bs"], z["nrhs"], z["na"], z["pb"]
    ab, a, p = z["ab"], z["a"], z["p"]
    me = lax.axis_index("row")
    mc = lax.axis_index("col")
    par = lax.rem(me, 2)
    zi = me // 2
    partner = me + 1 - 2 * par
    core = lax.rem(mc, 2)
    yi = mc // 2
    ny = m // 2
    twin = mc + 1 - 2 * core
    o_pan, o_l0, o_l1, o_p0, o_p1 = 0, pb, pb + na, pb + 2 * na, pb + 2 * na + cap

    paired = nz & (nz - 1) == 0

    def across(j, back=False):
        if not paired:
            return lax.rem(zi + (nz - j if back else j), nz)
        place, bit = zi, 1
        while bit < nz:
            if j & bit:
                place = place + bit * (1 - 2 * lax.rem(zi // bit, 2))
            bit *= 2
        return place

    counter = [0]
    pending = []

    def send(src, dst, axis, place, slot):
        cp = pltpu.make_async_remote_copy(
            src_ref=src, dst_ref=dst, send_sem=ssem.at[slot], recv_sem=rsem.at[slot],
            device_id={axis: place}, device_id_type=MESH,
        )
        cp.start()
        pending.append(cp)
        return cp

    def settle(count):
        for cp in pending[:count]:
            cp.wait_send()
        del pending[:count]

    def take(count):
        base = counter[0]
        counter[0] += count
        return base

    def span(block, size):
        return pl.ds(pl.multiple_of(block * size, size), size)

    def rows(ref, block, size):
        return ref.at[span(block, size)]

    def get(ref, block, size):
        return ref[span(block, size), :]

    def put(ref, block, size, value):
        ref[span(block, size), :] = value

    class RowSum:
        def __init__(self, part, size, xr, zs, zr):
            self.part, self.size = part, size
            self.xr, self.zs, self.zr = xr, zs, zr
            self.xk, self.zk = take(nz), take(nz)
            self.xc, self.zc = {}, {}

        def send_x(self, j):
            zd = across(j)
            self.xc[j] = send(
                rows(self.part, zd * 2 + 1 - par, self.size), self.xr.at[j], "row", partner,
                self.xk + j,
            )

        def forward(self):
            for j in order[:-1]:
                zd = across(j)
                self.xc[j].wait_recv()
                mine = get(self.part, zd * 2 + par, self.size)
                self.zs[j] = (mine.astype(F32) + self.xr[j].astype(F32)).astype(BF)
                self.zc[j] = send(
                    self.zs.at[j], self.zr.at[j], "row", zd * 2 + par, self.zk + j
                )

        def finish(self):
            self.xc[0].wait_recv()
            total = get(self.part, me, self.size).astype(F32) + self.xr[0].astype(F32)
            for j in order[:-1]:
                self.zc[j].wait_recv()
                total = total + self.zr[j].astype(F32)
            return total

    class RowGather:
        def __init__(self, full, size):
            self.full, self.size = full, size
            self.xk, self.zk = take(nz), take(nz)
            self.xc, self.zc = {}, {}

        def start(self):
            mine = rows(self.full, me, self.size)
            for j in order[:-1]:
                self.zc[j] = send(mine, mine, "row", across(j) * 2 + par, self.zk + j)
            self.xc[0] = send(mine, mine, "row", partner, self.xk)

        def forward(self):
            for j in order[:-1]:
                self.zc[j].wait_recv()
                theirs = rows(self.full, across(j, True) * 2 + par, self.size)
                self.xc[j] = send(theirs, theirs, "row", partner, self.xk + j)
            self.xc[0].wait_recv()

        def finish(self):
            for j in order[:-1]:
                self.xc[j].wait_recv()

    class ColSum:
        def __init__(self, part, landing, size):
            self.part, self.landing, self.size = part, landing, size
            self.s = take(m)
            self.c = {}

        def send_to(self, d):
            place = lax.rem(mc + d, m)
            self.c[d] = send(
                rows(self.part, place, self.size), self.landing.at[d], "col", place, self.s + d
            )

        def finish(self):
            total = get(self.part, mc, self.size).astype(F32)
            for d in range(1, m):
                self.c[d].wait_recv()
                total = total + self.landing[d].astype(F32)
            return total

    class ColGather:
        def __init__(self, full, size):
            self.full, self.size = full, size
            self.s, self.t = take(ny), take(ny)
            self.y, self.c = {}, {}

        def start(self):
            mine = rows(self.full, mc, self.size)
            for d in range(1, ny):
                place = lax.rem(yi + d, ny) * 2 + core
                self.y[d] = send(mine, mine, "col", place, self.s + d)
            self.c[0] = send(mine, mine, "col", twin, self.t)

        def forward(self):
            for d in range(1, ny):
                self.y[d].wait_recv()
                theirs = rows(self.full, lax.rem(yi + ny - d, ny) * 2 + core, self.size)
                self.c[d] = send(theirs, theirs, "col", twin, self.t + d)

        def finish(self):
            for d in range(ny):
                self.c[d].wait_recv()

    hp = p // 4

    class ColReduce:
        def __init__(self, part, full, twin_in, out, landing):
            self.part, self.full, self.twin_in = part, full, twin_in
            self.out, self.landing = out, landing
            self.s = take(2 + ny)
            self.c = {}

        def send_twin(self):
            self.t = send(
                rows(self.part, 1 - core, hp), self.twin_in, "col", twin, self.s
            )

        def send_y(self, mine):
            self.t.wait_recv()
            self.out[...] = (mine + self.twin_in[...].astype(F32)).astype(BF)
            for d in range(1, ny):
                place = lax.rem(yi + d, ny) * 2 + core
                self.c[d] = send(self.out, self.landing.at[d], "col", place, self.s + 1 + d)

        def total(self):
            total = self.out[...].astype(F32)
            for d in range(1, ny):
                self.c[d].wait_recv()
                total = total + self.landing[d].astype(F32)
            return total

        def share(self, value):
            put(self.full, core, hp, value)
            mine = rows(self.full, core, hp)
            self.g = send(mine, mine, "col", twin, self.s + 1)

        def finish(self):
            self.g.wait_recv()

    hb, hq, hn = b // 2, q // 2, nrhs // 2

    def pack(value, size):
        blocks = value.reshape(-1, size, hn)
        half = size // 2
        both = jnp.concatenate([blocks[:, :half], blocks[:, half:]], axis=2)
        return both.reshape(-1, nrhs)

    def unpack(value, size):
        half = size // 2
        blocks = value.astype(F32).reshape(-1, half, nrhs)
        both = jnp.concatenate([blocks[:, :, :hn], blocks[:, :, hn:]], axis=1)
        return both.reshape(-1, hn)

    def both_of(v0, v1, size):
        half = size // 2
        p0, p1 = (v.astype(F32).reshape(-1, half, nrhs) for v in (v0, v1))
        top = jnp.concatenate([p0[:, :, :hn], p1[:, :, :hn]], axis=2)
        low = jnp.concatenate([p0[:, :, hn:], p1[:, :, hn:]], axis=2)
        return jnp.concatenate([top, low], axis=1).reshape(-1, nrhs)

    def part_of(value, h):
        return value[:, h * hn:(h + 1) * hn]

    order = list(range(nz - 1, -1, -1))
    tile = max(min(256, cc), b)
    tiles = cc // tile

    def theirs_at(j):
        return across(j) * 2 + 1 - par

    def mine_at(j):
        return across(j) * 2 + par

    places = [theirs_at(j) for j in order] + [mine_at(j) for j in order]
    early = [mine_at(j) for j in order] + [partner]
    late = [theirs_at(j) for j in order[:-1]]

    load_x0 = pltpu.make_async_copy(prhs_hbm.at[0], prhs.at[0], lsem.at[0])
    load_ids = pltpu.make_async_copy(ids_hbm, ids, lsem.at[1])
    load_a = pltpu.make_async_copy(asol_hbm, known.at[pl.ds(mc * ab, ab)], lsem.at[2])
    load_b1 = pltpu.make_async_copy(b_hbm.at[1], vb1, lsem.at[3])
    load_b0 = pltpu.make_async_copy(b_hbm.at[0], vb0.at[pl.ds(0, cap)], lsem.at[4])
    load_d1 = pltpu.make_async_copy(d_hbm.at[1], vd1, lsem.at[5])
    load_x1 = pltpu.make_async_copy(prhs_hbm.at[1], prhs.at[1], lsem.at[6])
    load_r = pltpu.make_async_copy(arhs_hbm, arhs, lsem.at[7])
    load_d0 = [
        pltpu.make_async_copy(rows(d_hbm.at[0], place, b), rows(vd0, place, b), dsem.at[i])
        for i, place in enumerate(places)
    ]

    barrier = pltpu.get_barrier_semaphore()
    peers = [{"row": mine_at(j)} for j in range(1, nz)]
    peers += [{"row": partner}]
    peers += [{"col": lax.rem(mc + d, m)} for d in range(1, m)]
    for peer in peers:
        pl.semaphore_signal(barrier, inc=1, device_id=peer, device_id_type=MESH)
    load_x0.start()
    for load in load_d0:
        load.start()
    load_a.start()
    load_ids.start()

    sum_f0 = [RowSum(part_f0.at[h], hb, xr.at[0, h], zs.at[0, h], zr.at[0, h]) for h in range(2)]
    sum_f1 = [RowSum(part_f1.at[h], hb, xr.at[1, h], zs.at[1, h], zr.at[1, h]) for h in range(2)]
    sum_b0 = [RowSum(part_b0.at[h], hb, xr.at[2, h], zs.at[2, h], zr.at[2, h]) for h in range(2)]
    sum_b1 = RowSum(part_b1, b, xr1, zs1, zr1)
    gather_f0 = [RowGather(full_f0.at[h], hb) for h in range(2)]
    gather_b1 = [RowGather(full_b1.at[h], hb) for h in range(2)]
    gather_b0 = [RowGather(full_b0.at[h], hb) for h in range(2)]
    gather_f1 = RowGather(full_f1, b)
    col_p = [
        ColReduce(part_p.at[h], full_p.at[h], cl.at[0, h], ys.at[0, h], yl.at[0, h])
        for h in range(2)
    ]
    col_s1 = [
        ColReduce(part_s1.at[h], full_s1.at[h], cl.at[1, h], ys.at[1, h], yl.at[1, h])
        for h in range(2)
    ]
    sum_s0 = [ColSum(part_s0.at[h], cr.at[h], hq) for h in range(2)]
    sum_u = ColSum(part_u, cru, a)
    gather_a = ColGather(known, ab)

    def first(i):
        load_d0[i].wait()
        place = places[i]
        value = jnp.dot(get(vd0, place, b), x0, preferred_element_type=F32)
        for h in range(2):
            put(part_f0.at[h], place, hb, pack(part_of(value, h), b).astype(BF))

    load_x0.wait()
    x0 = prhs[0]
    for i in range(nz):
        first(i)
    for load in (load_b1, load_b0, load_d1, load_x1, load_r):
        load.start()
    def find(which, start, count, base):
        def step(k, carry):
            slot = jnp.int32(cap)
            for s in range(cap):
                slot = jnp.where(ids[which, s] == start + k, s, slot)
            idx[base + k] = slot
            return carry

        lax.fori_loop(0, count, step, 0)

    def prepare():
        known_t[na] = jnp.zeros((nrhs, bs), BF)
        vb0[cap] = jnp.zeros((bs, cc), BF)
        slots[0, cap] = jnp.zeros((bs, nrhs), F32)
        slots[1, cap] = jnp.zeros((bs, nrhs), F32)
        load_ids.wait()
        find(0, me * pb, pb, o_pan)
        for which, base in ((0, o_p0), (1, o_p1)):
            for s in range(cap):
                position = ids[which, s] - z["pw"] - me * na
                inside = jnp.logical_and(position >= 0, position < na)
                idx[base + s] = jnp.where(inside, position, na)

    def find_later(which):
        find(which, z["pw"] + me * na, na, (o_l0, o_l1)[which])

    def turn(side):
        def step(i, carry):
            at = ((i // ab) * 2 + side) * ab + i % ab
            known_t[at] = known[at].astype(F32).T.astype(BF)
            return carry

        lax.fori_loop(0, na // 2, step, 0)

    def gather_values(which, offset):
        for s in range(cap):
            vt[which, :, s * bs:(s + 1) * bs] = known_t[idx[offset + s]]

    def back_tile(which, vb, t):
        cols = span(t, tile)
        return jnp.dot(
            vt[which], vb[0:cap, :, cols].reshape(cap * bs, tile),
            preferred_element_type=F32,
        )

    def one_tiles(lo, hi):
        def step(t, carry):
            put(part_b1, t, tile, back_tile(1, vb1, t).T.astype(BF))
            return carry

        lax.fori_loop(lo, hi, step, 0)

    def zero_tiles(lo, hi):
        def step(t, carry):
            acc_t[:, span(t, tile)] = back_tile(0, vb0, t)
            return carry

        lax.fori_loop(lo, hi, step, 0)

    group = 2 if cap % 2 == 0 else 1
    groups = cap // group

    def later(which, vb, lo, hi):
        def step(t, carry):
            block = vb[pl.ds(t * group, group)].reshape(group * bs, cc)
            value = jnp.dot(block, wide[which], preferred_element_type=F32)
            slots[which, pl.ds(t * group, group)] = value.reshape(group, bs, nrhs)
            return carry

        lax.fori_loop(lo, hi, step, 0)

    fine_rows = b % 128 == 0
    fine_cols = q % 128 == 0
    steps_p = max(1, min(2, pb // 2))
    halves_p = (pb // 2) // steps_p

    def blocks_of(ref, found, size):
        return jnp.concatenate([get(ref, place, size) for place in found], axis=0)

    def panel_slots(half, t, some):
        found = []
        for i in range(steps_p):
            slot = idx[o_pan + half * (pb // 2) + t * steps_p + i]
            if some is None:
                found.append(vb0[slot])
            else:
                found.append(jnp.concatenate(
                    [vb0[slot, :, span(place, b)] for place in some], axis=1
                ))
        return jnp.concatenate(found, axis=0)

    tile_p = steps_p * bs

    def panel_first():
        x = both_of(*(blocks_of(full_f0.at[h], early, hb) for h in range(2)), b).astype(BF)
        for half in range(2):
            for t in range(halves_p):
                value = jnp.dot(panel_slots(half, t, early), x, preferred_element_type=F32)
                for h in range(2):
                    at = pl.ds((half * halves_p + t) * tile_p, tile_p)
                    acc_p[h, at, :] = part_of(value, h)

    def panel_rest(h):
        if fine_rows:
            x = unpack(blocks_of(full_f0.at[h], late, hb), b).astype(BF)
        else:
            x = unpack(full_f0[h], b).astype(BF)

        def one(half, t):
            value = jnp.dot(
                panel_slots(half, t, late if fine_rows else None), x,
                preferred_element_type=F32,
            )
            if fine_rows:
                value = value + acc_p[h, span(half * halves_p + t, tile_p), :]
            return pack(value, q)

        red = col_p[h]
        for t in range(halves_p):
            put(part_p.at[h], (1 - core) * halves_p + t, tile_p // 2, one(1 - core, t).astype(BF))
        red.send_twin()
        red.send_y(jnp.concatenate([one(core, t) for t in range(halves_p)], axis=0))

    def solve_forward(h):
        cols = [span(core, p // 2), span(1 - core, p // 2)]
        x = unpack(get(full_p.at[h], core, hp), q).astype(BF)
        for place in places:
            value = jnp.dot(vd1[span(place, b), cols[0]], x, preferred_element_type=F32)
            acc_f[h, span(place, b), :] = value
        if h == 0:
            sum_b1.forward()
        col_p[h].finish()
        x = unpack(get(full_p.at[h], 1 - core, hp), q).astype(BF)
        for i, place in enumerate(places):
            value = jnp.dot(vd1[span(place, b), cols[1]], x, preferred_element_type=F32)
            value = value + acc_f[h, span(place, b), :]
            put(part_f1.at[h], place, hb, pack(value, b).astype(BF))
            if i < nz:
                sum_f1[h].send_x(order[i])

    def back_first(full, vd):
        x = both_of(*(blocks_of(full.at[h], early, hb) for h in range(2)), b)
        acc_s[...] = jnp.dot(
            x.T.astype(BF), blocks_of(vd, early, b), preferred_element_type=F32
        )

    def back_input(h, full):
        return unpack(blocks_of(full.at[h], late, hb), b).T.astype(BF)

    def back_columns(h, xt, vd, cols):
        block = jnp.concatenate([vd[span(place, b), cols] for place in late], axis=0)
        yt = acc_s[h * hn:(h + 1) * hn, cols] + jnp.dot(xt, block, preferred_element_type=F32)
        return pack(yt.T, q)

    def solve_back_one(h):
        xt = back_input(h, full_b1)
        red = col_s1[h]
        put(part_s1.at[h], 1 - core, hp,
            back_columns(h, xt, vd1, span(1 - core, p // 2)).astype(BF))
        red.send_twin()
        red.send_y(back_columns(h, xt, vd1, span(core, p // 2)))

    def solve_back_zero(h):
        xt = back_input(h, full_b0)
        dests = sorted(range(1, m), key=lambda d: d % 2) + [0]
        if fine_cols:
            for d in dests:
                place = lax.rem(mc + d, m)
                put(part_s0.at[h], place, hq,
                    back_columns(h, xt, vd0, span(place, q)).astype(BF))
                if d:
                    sum_s0[h].send_to(d)
        else:
            part_s0[h] = back_columns(h, xt, vd0, pl.ds(0, p)).astype(BF)
            for d in range(1, m):
                sum_s0[h].send_to(d)

    def panel_columns(half, cols):
        return jnp.concatenate(
            [vb0[idx[o_pan + half * (pb // 2) + i], :, cols] for i in range(pb // 2)], axis=0
        )

    def panel_back(h):
        lanes = slice(h * hn, (h + 1) * hn)
        fine = tile == b
        order_t = places if fine else list(range(tiles))
        st = unpack(get(full_s1.at[h], core, hp), q).T.astype(BF)
        for t in order_t:
            cols = span(t, tile)
            value = jnp.dot(st, panel_columns(core, cols), preferred_element_type=F32)
            acc_t[lanes, cols] = acc_t[lanes, cols] + value
        col_s1[h].finish()
        st = unpack(get(full_s1.at[h], 1 - core, hp), q).T.astype(BF)
        for i, t in enumerate(order_t):
            cols = span(t, tile)
            value = jnp.dot(st, panel_columns(1 - core, cols), preferred_element_type=F32)
            value = (value + acc_t[lanes, cols]).T
            put(part_b0.at[h], t, tile // 2, pack(value, b).astype(BF))
            if fine and i < nz:
                sum_b0[h].send_x(order[i])
        if not fine:
            for j in order:
                sum_b0[h].send_x(j)

    def chain(h):
        sum_f0[h].forward()
        yield
        put(full_f0.at[h], me, hb, sum_f0[h].finish().astype(BF))
        gather_f0[h].start()
        yield
        gather_f0[h].forward()
        if h == 1:
            load_b0.wait()
            if fine_rows:
                panel_first()
        yield
        gather_f0[h].finish()
        panel_rest(h)
        yield
        mine = pack(part_of(prhs[1, span(core, p // 2), :].astype(F32), h), q)
        col_p[h].share((mine - col_p[h].total()).astype(BF))
        solve_forward(h)
        yield
        sum_f1[h].forward()
        yield
        f1_mine = sum_f1[h].finish().astype(BF)
        put(full_b1.at[h], me, hb, (f1_mine.astype(F32) - b1_mine[h]).astype(BF))
        gather_b1[h].start()
        put(full_f1, me * 2 + h, hb, f1_mine)
        yield
        gather_b1[h].forward()
        if h == 1:
            back_first(full_b1, vd1)
        yield
        gather_b1[h].finish()
        solve_back_one(h)
        yield
        col_s1[h].share(col_s1[h].total().astype(BF))
        panel_back(h)
        yield
        sum_b0[h].forward()
        yield
        b0_mine = sum_b0[h].finish()
        f0_mine = get(full_f0.at[h], me, hb).astype(F32)
        put(full_b0.at[h], me, hb, (f0_mine - b0_mine).astype(BF))
        gather_b0[h].start()
        yield
        gather_b0[h].forward()
        if h == 1:
            back_first(full_b0, vd0)
        yield
        gather_b0[h].finish()
        solve_back_zero(h)
        yield

    def widen(which, full):
        if which == 0:
            parts = [full_f0[h] for h in range(2)]
        else:
            blocks = full_f1[...].reshape(n, 2, hb, nrhs)
            parts = [blocks[:, h].reshape(n * hb, nrhs) for h in range(2)]
        wide[which] = both_of(*parts, b).astype(BF)

    def send_b1():
        for j in order:
            sum_b1.send_x(j)

    def finish_b1():
        total = sum_b1.finish()
        for h in range(2):
            b1_mine[h] = pack(part_of(total, h), b)

    def begin_one():
        gather_f1.finish()
        widen(1, full_f1)

    def add_update():
        for k in range(na):
            value = slots[0, idx[o_l0 + k]] + slots[1, idx[o_l1 + k]]
            part_u[k * bs:(k + 1) * bs, :] = value.astype(BF)
        for d in range(1, m):
            sum_u.send_to(d)

    def save_one():
        halves = [unpack(get(full_s1.at[h], mc, hq), q).astype(BF) for h in range(2)]
        sol[1] = jnp.concatenate(halves, axis=1)
        save_s1.start()

    def finish_update():
        load_r.wait()
        upd[...] = (arhs[...].astype(F32) - sum_u.finish()).astype(BF)
        save_u.start()

    save_s1 = pltpu.make_async_copy(sol.at[1], sol_hbm.at[1], osem.at[0])
    save_s0 = pltpu.make_async_copy(sol.at[0], sol_hbm.at[0], osem.at[1])
    save_u = pltpu.make_async_copy(upd, upd_hbm, osem.at[2])

    call = functools.partial

    def piece(work, total, lo, hi, parts=8):
        return call(work, lo * total // parts, hi * total // parts)

    ones, zeros = call(piece, one_tiles, tiles), call(piece, zero_tiles, tiles)
    later_0 = call(piece, call(later, 0, vb0), groups)
    later_1 = call(piece, call(later, 1, vb1), groups)
    side = {
        (0, 1): [gather_a.forward, call(turn, core)],
        (1, 0): [gather_a.finish, call(turn, 1 - core), call(gather_values, 1, o_p1)],
        (1, 1): [load_b1.wait, ones(0, 4)],
        (2, 0): [ones(4, 6)],
        (2, 1): [ones(6, 8), send_b1],
        (3, 0): [call(gather_values, 0, o_p0)],
        (3, 1): [call(widen, 0, None), later_0(0, 1), load_d1.wait, load_x1.wait],
        (4, 0): [later_0(1, 3)],
        (4, 1): [later_0(3, 6)],
        (5, 0): [later_0(6, 8)],
        (5, 1): [finish_b1, zeros(0, 1)],
        (6, 0): [zeros(1, 3)],
        (6, 1): [gather_f1.start, zeros(3, 5)],
        (7, 0): [zeros(5, 6)],
        (7, 1): [zeros(6, 7)],
        (8, 0): [gather_f1.forward, zeros(7, 8)],
        (9, 1): [save_one],
        (10, 0): [begin_one, later_1(0, 1)],
        (10, 1): [later_1(1, 4)],
        (11, 0): [later_1(4, 6)],
        (11, 1): [later_1(6, 8), add_update],
        (13, 1): [finish_update],
    }
    pl.semaphore_wait(barrier, len(peers))
    for h in range(2):
        for j in order[:-1]:
            sum_f0[h].send_x(j)
    load_a.wait()
    gather_a.start()
    for h in range(2):
        sum_f0[h].send_x(0)
    for i in range(nz, 2 * nz):
        first(i)
    prepare()
    find_later(0)
    find_later(1)
    chains = [chain(0), chain(1)]
    sent = []
    for it in range(14):
        for h in range(2):
            next(chains[h])
            for task in side.get((it, h), ()):
                task()
        sent.append(len(pending))
        if it >= 2:
            count = sent[it - 2]
            settle(count)
            sent = [s - count for s in sent]

    halves = [unpack(sum_s0[h].finish(), q).astype(BF) for h in range(2)]
    sol[0] = jnp.concatenate(halves, axis=1)
    save_s0.start()
    settle(len(pending))
    save_s1.wait()
    save_u.wait()
    save_s0.wait()


def hand_over(sol, upd, sol_out, upd_out, sol_held, upd_held, sem):
    loads = [
        pltpu.make_async_copy(sol, sol_held, sem.at[0]),
        pltpu.make_async_copy(upd, upd_held, sem.at[1]),
    ]
    saves = [
        pltpu.make_async_copy(sol_held, sol_out, sem.at[2]),
        pltpu.make_async_copy(upd_held, upd_out, sem.at[3]),
    ]
    for load in loads:
        load.start()
    for load, save in zip(loads, saves):
        load.wait()
        save.start()
    for save in saves:
        save.wait()


def on_device(diag, panel_rhs, below, row_ids, ancestor_rhs, ancestor_solution):
    n, m = lax.axis_size("row"), lax.axis_size("col")
    z = sizes_of(n, m, diag, panel_rhs, below, row_ids, ancestor_rhs)
    nz, b, q = z["nz"], z["b"], z["q"]
    cc, p, cap, bs, nrhs, na, pb = (z[k] for k in ("cc", "p", "cap", "bs", "nrhs", "na", "pb"))
    a, ab, hn, ny = z["a"], z["ab"], z["nrhs"] // 2, m // 2

    hbm = pl.BlockSpec(memory_space=pl.ANY)
    nsem = 14 * 2 * nz + 4 * (2 + ny) + 4 * m + 2 * ny
    V = pltpu.VMEM
    shapes = (
        jax.ShapeDtypeStruct((2, q, nrhs), BF),
        jax.ShapeDtypeStruct((a, nrhs), BF),
    )
    made = pl.pallas_call(
        functools.partial(kernel, z),
        out_shape=shapes,
        in_specs=[hbm] * 6,
        out_specs=(hbm, hbm),
        scratch_shapes=[
            pltpu.SMEM((2, cap), jnp.int32), pltpu.SMEM((pb + 2 * na + 2 * cap,), jnp.int32),
            V((cc, p), BF), V((cc, p), BF),
            V((cap + 1, bs, cc), BF), V((cap, bs, cc), BF),
            V((2, p, nrhs), BF), V((a, nrhs), BF), V((2, q, nrhs), BF), V((a, nrhs), BF),
            V((na, bs, nrhs), BF), V((na + 1, nrhs, bs), BF), V((2, nrhs, cap * bs), BF),
            V((2, cap + 1, bs, nrhs), F32), V((nrhs, cc), F32),
            V((2, p, hn), F32), V((2, cc, hn), F32), V((nrhs, p), F32), V((2, b // 2, nrhs), F32),
            V((cc, nrhs), BF), V((cc, nrhs), BF), V((2, cc, nrhs), BF),
        ] + [V((2, cc // 2, nrhs), BF)] * 6 + [V((3, 2, nz, b // 2, nrhs), BF)] * 3 + [
            V((nz, b, nrhs), BF)
        ] * 3 + [V((2, p // 2, nrhs), BF)] * 5 + [
            V((na * bs, nrhs), BF),
            V((2, 2, p // 4, nrhs), BF), V((2, 2, p // 4, nrhs), BF),
            V((2, 2, ny, p // 4, nrhs), BF),
            V((2, m, q // 2, nrhs), BF), V((m, a, nrhs), BF),
            pltpu.SemaphoreType.DMA((8,)),
            pltpu.SemaphoreType.DMA((n,)),
            pltpu.SemaphoreType.DMA((3,)),
            pltpu.SemaphoreType.DMA((nsem,)),
            pltpu.SemaphoreType.DMA((nsem,)),
        ],
        compiler_params=pltpu.CompilerParams(
            collective_id=0, has_side_effects=True, vmem_limit_bytes=62 * 1024 * 1024
        ),
    )(
        row_ids, diag, panel_rhs, below.reshape(2, cap, bs, cc), ancestor_rhs,
        ancestor_solution.reshape(ab, bs, nrhs),
    )
    return pl.pallas_call(
        hand_over,
        out_shape=shapes,
        in_specs=[hbm] * 2,
        out_specs=(hbm, hbm),
        scratch_shapes=[V(s.shape, s.dtype) for s in shapes] + [pltpu.SemaphoreType.DMA((4,))],
    )(*made)


def solution(mesh):
    in_specs = (
        P(None, "col", "row"),
        P(None, "row", None),
        P(None, "row", "col"),
        P(None, "row"),
        P(("row", "col"), None),
        P(("row", "col"), None),
    )
    out_specs = (P(None, ("row", "col"), None), P(("row", "col"), None))
    return jax.shard_map(
        on_device, mesh=mesh, in_specs=in_specs, out_specs=out_specs, check_vma=False
    )
```
